32 devices in a mesh: gx: 8 (over y, x, core), gy: 4 (over z).
Axes of the slice: x: 2, y: 2, z: 4, core: 2. Of those that a mesh axis runs over, the one named last changes fastest.
Arguments:
- positions: float32 [3, 8, 4, 128], P(None, 'gx', 'gy'), may hold values from 0 to 384, as said below
- neighbours: int32 [32, 8, 4, 128], P(None, 'gx', 'gy'), may hold values from 0 to 1151, as said below
- live_count: int32 [8, 4], P('gx', 'gy'), may hold values from 16 to 128, as said below
- stencil_base: int32 [3, 8, 4, 128], P(None, 'gx', 'gy'), may hold values from -1 to 383, as said below
- spline_weight: float32 [3, 4, 8, 4, 128], P(None, None, 'gx', 'gy'), may hold values from 0 to 1, as said below
- spline_slope: float32 [3, 4, 8, 4, 128], P(None, None, 'gx', 'gy'), may hold values from -1 to 1, as said below
- embed_scale: float32 [100], replicated, may hold values from -12 to 12
- embed_bias: float32 [100], replicated, may hold values from -4 to 4
- desc_gain: float32 [1600], replicated, may hold values from 0.25 to 1.75
- fit_in: bfloat16 [128, 1600], replicated, may hold values from -0.15625 to 0.15625
- fit_bias: float32 [128], replicated, may hold values from -3 to 3
- fit_hidden: bfloat16 [128, 128], replicated, may hold values from -0.5 to 0.5
- fit_bias_two: float32 [128], replicated, may hold values from -3 to 3
- fit_out: float32 [128], replicated, may hold values from -0.5 to 0.5
Outputs:
- centroid_energy: float32 [8, 4, 128], P('gx', 'gy')
- centroid_force: float32 [3, 8, 4, 128], P(None, 'gx', 'gy')
The draws below stay inside these ranges and needn't reach their ends.
Inputs may be any that keep to these rules, and one draw needn't show every extreme that they name: `live_count`: slots below a column's count are live; some column has all 128 slots live. `neighbours`: every entry names a live slot of one of the nine blocks of the column's neighbourhood. `stencil_base`: along x the base lies in -1 to 46, along y in -1 to 94, along z in 0 to 383. `positions`: x lies in 0 to 48, y in 0 to 96, z in 0 to 384. `spline_weight`: cubic B-spline weights of a fraction in [0, 1) for each axis; the four weights sum to one. `spline_slope`: the derivatives of those weights with respect to the fraction.
All inputs are finite; a program needn't handle non-finite values.
Results may differ from the reference program's by a relative error of at most 0.006.
The reference program's roundings to bfloat16 on the way (of `normed`) count: a program that leaves them out, or rounds other values in their place, can miss the bound.
Values sent between devices are 32-bit elements; how exact they have to be, the bound alone decides.
A program may use at most 128 MiB of HBM per device.

```python
import math
import jax
import jax.numpy as jnp
from jax import lax

GRID = 384
EMB = 100
AXIS = 16
FIT = 128
NEIGH = 32
ATOM_DEV = 128
DESC = 1600
CX = 48
CY = 96
N_GX = 8
N_GY = 4


def live_counts(key):
    fewest = ATOM_DEV // 8
    spread_range = ATOM_DEV - fewest
    picked = jax.random.randint(jax.random.fold_in(key, 101), (N_GX, N_GY), 0, spread_range + 1)
    counts = fewest + picked * picked // spread_range
    fullest = jax.random.randint(jax.random.fold_in(key, 102), (), 0, N_GX * N_GY)
    flat = jnp.where(jnp.arange(N_GX * N_GY) == fullest, ATOM_DEV, counts.reshape(-1))
    return flat.reshape(N_GX, N_GY).astype(jnp.int32)


def draw_live_count(key, part):
    return live_counts(key)


def draw_neighbours(key, part):
    counts = live_counts(key)
    shape = (NEIGH, N_GX, N_GY, ATOM_DEV)
    block = jax.random.randint(jax.random.fold_in(key, 103), shape, 0, 9)
    stride_x = block // 3 - 1
    stride_y = block % 3 - 1
    rows = lax.broadcasted_iota(jnp.int32, shape, 1)
    cols = lax.broadcasted_iota(jnp.int32, shape, 2)
    slots = lax.broadcasted_iota(jnp.int32, shape, 3)
    other = counts[(rows + stride_x) % N_GX, (cols + stride_y) % N_GY]
    owned = counts[rows, cols]
    aligned = jnp.minimum(slots, owned - 1) * other // owned
    jitter = jax.random.randint(jax.random.fold_in(key, 104), shape, -3, 4)
    chosen = jnp.clip(aligned + jitter, 0, other - 1)
    return (block * ATOM_DEV + chosen).astype(jnp.int32)


def draw_positions(key, part):
    counts = live_counts(key)
    shape = (N_GX, N_GY, ATOM_DEV)
    fraction = jax.random.uniform(jax.random.fold_in(key, 105), (3,) + shape, jnp.float32)
    slots = lax.broadcasted_iota(jnp.int32, shape, 2)
    owned = counts[:, :, None]
    height = jnp.where(slots < owned, (slots.astype(jnp.float32) + fraction[2]) / owned.astype(jnp.float32), fraction[2])
    coord_x = fraction[0] * (GRID // N_GX)
    coord_y = fraction[1] * (GRID // N_GY)
    coord_z = jnp.minimum(height * GRID, GRID * 0.999)
    return jnp.stack([coord_x, coord_y, coord_z]).astype(jnp.float32)


def draw_stencil_base(key, part):
    shape = (N_GX, N_GY, ATOM_DEV)
    base_x = jax.random.randint(jax.random.fold_in(key, 107), shape, -1, GRID // N_GX - 1)
    base_y = jax.random.randint(jax.random.fold_in(key, 108), shape, -1, GRID // N_GY - 1)
    base_z = jax.random.randint(jax.random.fold_in(key, 109), shape, 0, GRID)
    return jnp.stack([base_x, base_y, base_z]).astype(jnp.int32)


def spline_fraction(key):
    fraction = jax.random.uniform(jax.random.fold_in(key, 106), (3, N_GX, N_GY, ATOM_DEV), jnp.float32)
    return fraction


def draw_spline_weight(key, part):
    fraction = spline_fraction(key)
    remain = 1.0 - fraction
    cube = fraction * fraction * fraction
    square = fraction * fraction
    values = [remain * remain * remain / 6.0, (3.0 * cube - 6.0 * square + 4.0) / 6.0, (-3.0 * cube + 3.0 * square + 3.0 * fraction + 1.0) / 6.0, cube / 6.0]
    return jnp.stack(values, axis=1).astype(jnp.float32)


def draw_spline_slope(key, part):
    fraction = spline_fraction(key)
    remain = 1.0 - fraction
    square = fraction * fraction
    values = [-0.5 * remain * remain, (3.0 * square - 4.0 * fraction) / 2.0, (-3.0 * square + 2.0 * fraction + 1.0) / 2.0, 0.5 * square]
    return jnp.stack(values, axis=1).astype(jnp.float32)


def normal_values(stream_key, shape, spread, limit, kind=jnp.bfloat16):
    values = jax.random.normal(stream_key, shape, jnp.float32) * spread
    return jnp.minimum(jnp.maximum(values, -limit), limit).astype(kind)


def setup_inputs(seed: int = 0) -> dict:
    keys = jax.random.split(jax.random.key(seed), 15)
    return {
        "positions": draw_positions(jax.random.fold_in(keys[14], 71), 0),
        "neighbours": draw_neighbours(jax.random.fold_in(keys[14], 71), 0),
        "live_count": draw_live_count(jax.random.fold_in(keys[14], 71), 0),
        "stencil_base": draw_stencil_base(jax.random.fold_in(keys[14], 71), 0),
        "spline_weight": draw_spline_weight(jax.random.fold_in(keys[14], 71), 0),
        "spline_slope": draw_spline_slope(jax.random.fold_in(keys[14], 71), 0),
        "embed_scale": normal_values(keys[6], (EMB,), 3.0, 12.0, jnp.float32),
        "embed_bias": normal_values(keys[7], (EMB,), 1.0, 4.0, jnp.float32),
        "desc_gain": jnp.clip(1.0 + 0.15 * jax.random.normal(keys[8], (DESC,), jnp.float32), 0.25, 1.75),
        "fit_in": normal_values(keys[9], (FIT, DESC), DESC ** -0.5, 0.15625),
        "fit_bias": normal_values(keys[10], (FIT,), 0.5, 3.0, jnp.float32),
        "fit_hidden": normal_values(keys[11], (FIT, FIT), FIT ** -0.5, 0.5),
        "fit_bias_two": normal_values(keys[12], (FIT,), 0.5, 3.0, jnp.float32),
        "fit_out": normal_values(keys[13], (FIT,), FIT ** -0.5, 0.5, jnp.float32),
    }


highest = lax.Precision.HIGHEST
radius_scale = 4.0
screen_width = 0.25
norm_floor = 1e-06
full_turn = 2.0 * math.pi

def stencil_table(anchor, weights, length, offset, periodic):
    count = anchor.shape[0]
    cell_index = lax.broadcasted_iota(jnp.int32, (4, length, count), 1)
    tap_index = lax.broadcasted_iota(jnp.int32, (4, length, count), 0)
    target = anchor[None, None, :] + tap_index + offset
    if periodic:
        target = target % length
    chosen = jnp.where(target == cell_index, weights[:, None, :], jnp.zeros((), weights.dtype))
    return lax.optimization_barrier(jnp.sum(chosen, axis=0))

def spread_cells(charge, anchor, weights, extent_x, extent_y, offset, length):
    table_x = stencil_table(anchor[0], weights[0] * charge[None, :], extent_x, offset, False)
    table_y = stencil_table(anchor[1], weights[1], extent_y, offset, False)
    table_z = stencil_table(anchor[2], weights[2], length, 0, True)
    planes = (table_x[:, None, :] * table_y[None, :, :]).reshape(extent_x * extent_y, -1)
    return jnp.dot(planes, table_z.T, precision=highest).reshape(extent_x, extent_y, length)

def interpolate(padded, anchor, weights, slopes):
    extent_x, extent_y, length = padded.shape
    table_x = stencil_table(anchor[0], weights[0], extent_x, 2, False)
    slope_x = stencil_table(anchor[0], slopes[0], extent_x, 2, False)
    table_y = stencil_table(anchor[1], weights[1], extent_y, 2, False)
    slope_y = stencil_table(anchor[1], slopes[1], extent_y, 2, False)
    table_z = stencil_table(anchor[2], weights[2], length, 0, True)
    slope_z = stencil_table(anchor[2], slopes[2], length, 0, True)
    flat = padded.reshape(extent_x * extent_y, length)
    along = jnp.dot(flat, table_z, precision=highest).reshape(extent_x, extent_y, -1)
    slant = jnp.dot(flat, slope_z, precision=highest).reshape(extent_x, extent_y, -1)
    over_y = lax.optimization_barrier(jnp.sum(along * table_y[None], axis=1))
    value = lax.optimization_barrier(jnp.sum(table_x * over_y, axis=0))
    field_x = -lax.optimization_barrier(jnp.sum(slope_x * over_y, axis=0))
    over_x = lax.optimization_barrier(jnp.sum(along * table_x[:, None, :], axis=0))
    field_y = -lax.optimization_barrier(jnp.sum(slope_y * over_x, axis=0))
    slant_y = lax.optimization_barrier(jnp.sum(slant * table_y[None], axis=1))
    field_z = -lax.optimization_barrier(jnp.sum(table_x * slant_y, axis=0))
    return (value, jnp.stack([field_x, field_y, field_z]))

def fitted_charge(nearby, listed, count, embed_scale, embed_bias, desc_gain, fit_in, fit_bias, fit_hidden, fit_bias_two, fit_out):
    atoms = listed.shape[1]
    center = nearby[:, 4 * atoms:5 * atoms]
    picked = jnp.take(nearby, listed.reshape(-1), axis=1).reshape(3, listed.shape[0], atoms)
    delta = picked - center[:, None, :]
    radius = jnp.sqrt(lax.optimization_barrier(jnp.sum(delta * delta, axis=0)))
    smooth = 1.0 / (1.0 + radius / radius_scale)
    factor = smooth / (radius + radius_scale)
    envelope = jnp.concatenate([smooth[None], delta * factor[None]], axis=0)
    embed = jnp.tanh(smooth[None] * embed_scale[:, None, None] + embed_bias[:, None, None])
    mixed = jnp.einsum('ekn,ckn->ecn', embed, envelope, precision=highest)
    descriptor = jnp.einsum('ecn,acn->ean', mixed, mixed[:AXIS], precision=highest).reshape(-1, atoms)
    scaling = lax.rsqrt(lax.optimization_barrier(jnp.mean(descriptor * descriptor, axis=0)) + norm_floor)
    normed = (descriptor * scaling[None, :] * desc_gain[:, None]).astype(jnp.bfloat16)
    first = jnp.tanh(jnp.dot(fit_in, normed, preferred_element_type=jnp.float32) + fit_bias[:, None])
    second = jnp.tanh(jnp.dot(fit_hidden, first.astype(jnp.bfloat16), preferred_element_type=jnp.float32) + fit_bias_two[:, None]) + first
    charge = lax.optimization_barrier(jnp.sum(fit_out[:, None] * second, axis=0))
    slot_index = lax.broadcasted_iota(jnp.int32, (atoms,), 0)
    return jnp.where(slot_index < count, charge, jnp.zeros((), charge.dtype))

def wave_number(index, length):
    signed = jnp.where(index > length // 2, index - length, index)
    return signed.astype(jnp.float32) * (full_turn / length)

def green_values(index_x, index_y, index_z, length):
    wave_x = wave_number(index_x, length)
    wave_y = wave_number(index_y, length)
    wave_z = wave_number(index_z, length)
    square = wave_x * wave_x + wave_y * wave_y + wave_z * wave_z
    safe = jnp.where(square > 0, square, 1.0)
    value = 2.0 * full_turn * jnp.exp(-0.5 * screen_width * screen_width * square) / safe
    keep = (square > 0) & (index_z != length // 2)
    return jnp.where(keep, value, 0.0)

def fold_edges(padded, length):
    inner = padded[2:length + 2]
    inner = inner.at[0:2].add(padded[length + 2:length + 4])
    inner = inner.at[length - 2:length].add(padded[0:2])
    return inner

def reference(positions, neighbours, live_count, stencil_base, spline_weight, spline_slope, embed_scale, embed_bias, desc_gain, fit_in, fit_bias, fit_hidden, fit_bias_two, fit_out):
    blocks = []
    for stride_x in (-1, 0, 1):
        for stride_y in (-1, 0, 1):
            moved = jnp.roll(positions, (-stride_x, -stride_y), axis=(1, 2))
            offset = jnp.array([stride_x * CX, stride_y * CY, 0], dtype=positions.dtype)
            blocks.append(moved + offset[:, None, None, None])
    stacked = jnp.stack(blocks, axis=1)
    nearby = jnp.transpose(stacked, (2, 3, 0, 1, 4)).reshape(N_GX, N_GY, 3, 9 * ATOM_DEV)
    listed = jnp.transpose(neighbours, (1, 2, 0, 3))

    def one_column(nearby_one, listed_one, count_one):
        return fitted_charge(nearby_one, listed_one, count_one, embed_scale, embed_bias, desc_gain, fit_in, fit_bias, fit_hidden, fit_bias_two, fit_out)

    def one_row(items):
        return jax.vmap(one_column)(items[0], items[1], items[2])
    charges = lax.map(one_row, (nearby, listed, live_count))
    anchors = jnp.transpose(stencil_base, (1, 2, 0, 3))
    weights = jnp.transpose(spline_weight, (2, 3, 0, 1, 4))
    slopes = jnp.transpose(spline_slope, (2, 3, 0, 1, 4))

    def place(index, grid):
        row_index = (index // N_GY).astype(jnp.int32)
        col_index = (index % N_GY).astype(jnp.int32)
        cells = spread_cells(charges[row_index, col_index], anchors[row_index, col_index], weights[row_index, col_index], CX + 4, CY + 4, 2, GRID)
        start = (row_index * CX, col_index * CY, jnp.zeros((), jnp.int32))
        before = lax.dynamic_slice(grid, start, cells.shape)
        return lax.dynamic_update_slice(grid, before + cells, start)
    grid = lax.fori_loop(0, N_GX * N_GY, place, jnp.zeros((GRID + 4, GRID + 4, GRID), jnp.float32))
    grid = fold_edges(grid, GRID)
    density = jnp.swapaxes(fold_edges(jnp.swapaxes(grid, 0, 1), GRID), 0, 1)
    modes = jnp.arange(GRID, dtype=jnp.int32)
    green = green_values(modes[:, None, None], modes[None, :, None], modes[None, None, :], GRID)
    spectrum = jnp.fft.fftn(density) * green
    potential = jnp.real(jnp.fft.ifftn(spectrum)).astype(jnp.float32)
    padded = jnp.pad(potential, ((2, 2), (2, 2), (0, 0)), mode='wrap')

    def gather_one(index):
        row_index = (index // N_GY).astype(jnp.int32)
        col_index = (index % N_GY).astype(jnp.int32)
        start = (row_index * CX, col_index * CY, jnp.zeros((), jnp.int32))
        window = lax.dynamic_slice(padded, start, (CX + 4, CY + 4, GRID))
        value, field = interpolate(window, anchors[row_index, col_index], weights[row_index, col_index], slopes[row_index, col_index])
        charge = charges[row_index, col_index]
        return (0.5 * charge * value, charge[None, :] * field)
    energy, force = lax.map(gather_one, jnp.arange(N_GX * N_GY, dtype=jnp.int32))
    energy = energy.reshape(N_GX, N_GY, ATOM_DEV)
    force = jnp.transpose(force.reshape(N_GX, N_GY, 3, ATOM_DEV), (2, 0, 1, 3))
    return (energy, force)
```

```python
import math

import jax
import jax.numpy as jnp
from jax import lax
from jax.experimental import pallas as pl
from jax.experimental.pallas import tpu as pltpu
from jax.sharding import PartitionSpec as P

GRID = 384
AXIS = 16
LANES = 128
CHUNK = 512
TILE = 256

highest = lax.Precision.HIGHEST
radius_scale = 4.0
screen_width = 0.25
norm_floor = 1e-06
full_turn = 2.0 * math.pi


def charge_kernel(nearby_ref, listed_ref, scale_ref, bias_ref, mixed_ref, env_ref):
    neigh, atoms = listed_ref.shape
    listed = listed_ref[...]
    slot = listed % atoms
    block = listed // atoms
    square = jnp.zeros((neigh, atoms), jnp.float32)
    deltas = []
    for c in range(3):
        center = nearby_ref[c, 4:5, :]
        picked = jnp.zeros((neigh, atoms), jnp.float32)
        for b in range(9):
            row = jnp.broadcast_to(nearby_ref[c, b : b + 1, :], (neigh, atoms))
            got = jnp.take_along_axis(row, slot, axis=1, mode="promise_in_bounds")
            picked = jnp.where(block == b, got, picked)
        delta = picked - center
        deltas.append(delta)
        square = square + delta * delta
    radius = jnp.sqrt(square)
    smooth = 1.0 / (1.0 + radius / radius_scale)
    factor = smooth / (radius + radius_scale)
    env_ref[0] = smooth
    for c in range(3):
        env_ref[c + 1] = deltas[c] * factor
    mixed_ref[...] = jnp.zeros_like(mixed_ref)

    def step(k, carry):
        row = env_ref[0, pl.ds(k, 1), :]
        embed = jnp.tanh(row * scale_ref[...] + bias_ref[...])
        for c in range(4):
            mixed_ref[c] += embed * env_ref[c, pl.ds(k, 1), :]
        return carry

    lax.fori_loop(0, neigh, step, 0)


def mixed_features(nearby, listed, embed_scale, embed_bias):
    neigh, atoms = listed.shape
    width = embed_scale.shape[0]
    spread = jnp.broadcast_to(embed_scale[:, None], (width, atoms))
    shift = jnp.broadcast_to(embed_bias[:, None], (width, atoms))
    return pl.pallas_call(
        charge_kernel,
        out_shape=jax.ShapeDtypeStruct((4, width, atoms), jnp.float32),
        scratch_shapes=[pltpu.VMEM((4, neigh, atoms), jnp.float32)],
    )(nearby, listed, spread, shift)


def fit_charge(mixed, count, desc_gain, fit_in, fit_bias, fit_hidden, fit_bias_two, fit_out):
    atoms = mixed.shape[2]
    descriptor = jnp.sum(mixed[:, :, None, :] * mixed[:, None, :AXIS, :], axis=0).reshape(-1, atoms)
    scaling = lax.rsqrt(jnp.mean(descriptor * descriptor, axis=0) + norm_floor)
    normed = (descriptor * scaling[None, :] * desc_gain[:, None]).astype(jnp.bfloat16)
    first = jnp.tanh(
        jnp.dot(fit_in, normed, preferred_element_type=jnp.float32) + fit_bias[:, None]
    )
    second = (
        jnp.tanh(
            jnp.dot(fit_hidden, first.astype(jnp.bfloat16), preferred_element_type=jnp.float32)
            + fit_bias_two[:, None]
        )
        + first
    )
    charge = jnp.sum(fit_out[:, None] * second, axis=0)
    slot_index = lax.broadcasted_iota(jnp.int32, (atoms,), 0)
    return jnp.where(slot_index < count, charge, jnp.zeros((), charge.dtype))


def pack_kernel(count_ref, sites_ref, packed_ref):
    columns, rows, atoms = sites_ref.shape
    packed_ref[...] = jnp.zeros_like(packed_ref)
    lane = lax.broadcasted_iota(jnp.int32, (rows, atoms), 1)

    def step(j, start):
        count = count_ref[j]
        tile = start // atoms
        shift = start % atoms
        block = jnp.where(lane < count, sites_ref[j], 0.0)
        turned = pltpu.roll(block, shift, 1)
        packed_ref[tile] = packed_ref[tile] + jnp.where(lane >= shift, turned, 0.0)
        packed_ref[tile + 1] = jnp.where(lane < shift, turned, 0.0)
        return start + count

    lax.fori_loop(0, columns, step, 0)


def pack_sites(counts, sites):
    columns, rows, atoms = sites.shape
    return pl.pallas_call(
        pack_kernel,
        in_specs=[
            pl.BlockSpec(memory_space=pltpu.SMEM),
            pl.BlockSpec(memory_space=pltpu.VMEM),
        ],
        out_specs=pl.BlockSpec(memory_space=pltpu.VMEM),
        out_shape=jax.ShapeDtypeStruct((columns + 1, rows, atoms), jnp.float32),
    )(counts, sites)


def axis_waves(cell, start, groups):
    def turn(index):
        angle = ((index * cell[None, :]) % GRID).astype(jnp.float32) * (full_turn / GRID)
        return jnp.cos(angle), jnp.sin(angle)

    low_cos, low_sin = turn(jnp.arange(8, dtype=jnp.int32)[:, None])
    high_cos, high_sin = turn(start + 8 * jnp.arange(groups, dtype=jnp.int32)[:, None])
    low_cos, low_sin = low_cos[None], low_sin[None]
    high_cos, high_sin = high_cos[:, None], high_sin[:, None]
    cosine = high_cos * low_cos - high_sin * low_sin
    sine = high_sin * low_cos + high_cos * low_sin
    return cosine.reshape(groups * 8, -1), sine.reshape(groups * 8, -1)


def axis_table(cosine, sine, taps, start):
    count = cosine.shape[0]
    angle = (start + jnp.arange(count, dtype=jnp.int32)).astype(jnp.float32) * (full_turn / GRID)
    angle = angle[:, None]
    real = taps[1] + (taps[0] + taps[2]) * jnp.cos(angle) + taps[3] * jnp.cos(2.0 * angle)
    imag = (taps[2] - taps[0]) * jnp.sin(angle) + taps[3] * jnp.sin(2.0 * angle)
    return cosine * real - sine * imag, sine * real + cosine * imag


def plane_tables(cell, taps, slopes, start, groups):
    cosine, sine = axis_waves(cell, start, groups)
    parity = (1 - 2 * (cell % 2)).astype(jnp.float32)
    zero_mode = (start + jnp.arange(groups * 8, dtype=jnp.int32) == 0)[:, None]
    tables = []
    for row in (taps, slopes):
        even, odd = axis_table(cosine, sine, row, start)
        last = parity * (row[1] + row[3] - row[0] - row[2])
        tables.append(jnp.concatenate([even, jnp.where(zero_mode, last[None], odd)], axis=0))
    return tables


def plane_modes(start, count):
    mode = start + jnp.arange(count, dtype=jnp.int32)
    modes = jnp.concatenate([mode, jnp.where(mode == 0, GRID // 2, mode)])
    factor = jnp.where((modes == 0) | (modes == GRID // 2), 1.0, 2.0) / GRID
    wave = modes.astype(jnp.float32) * (full_turn / GRID)
    return wave * wave, factor.astype(jnp.float32)


def halves(table):
    high = lax.reduce_precision(table, 8, 7)
    low = table - high
    return jnp.concatenate([high, low], axis=0).astype(jnp.bfloat16)


def mesh_kernel(
    count_ref,
    squares_ref,
    factors_ref,
    square_y_ref,
    square_z_ref,
    charge_ref,
    x_ref,
    slope_x_ref,
    y_ref,
    slope_y_ref,
    z_ref,
    slope_z_ref,
    out_ref,
    spectrum_ref,
    scaled_ref,
    found_ref,
):
    modes_x = x_ref.shape[0]
    modes_y = y_ref.shape[0]
    depth = z_ref.shape[0]
    modes_z = depth // 2
    columns = out_ref.shape[0]
    group = 8
    total = lax.fori_loop(0, columns, lambda j, acc: acc + count_ref[j], 0)
    spectrum_ref[...] = jnp.zeros_like(spectrum_ref)

    def gather_chunk(chunk, carry):
        lanes = pl.ds(pl.multiple_of(chunk * CHUNK, CHUNK), CHUNK)
        y = y_ref[:, lanes] * charge_ref[:, lanes]
        high = z_ref[:modes_z, lanes]
        low = z_ref[modes_z:, lanes]

        def rows(g, inner):
            x = x_ref[pl.ds(pl.multiple_of(g * group, group), group), lanes]
            left = jnp.concatenate(
                [(x[a : a + 1] * y).astype(jnp.bfloat16) for a in range(group)], axis=0
            )
            where = pl.ds(pl.multiple_of(g * group * modes_y, group * modes_y), group * modes_y)
            form = (((1,), (1,)), ((), ()))
            spectrum_ref[where, :] += lax.dot_general(
                left, high, form, preferred_element_type=jnp.float32
            ) + lax.dot_general(left, low, form, preferred_element_type=jnp.float32)
            return inner

        return lax.fori_loop(0, modes_x // group, rows, carry)

    lax.fori_loop(0, (total + CHUNK - 1) // CHUNK, gather_chunk, 0)

    square_y = square_y_ref[:, 0:1]
    factor_y = square_y_ref[:, 1:2]
    square_z = square_z_ref[0:1, :]
    factor_z = square_z_ref[1:2, :]
    plane = square_y + square_z
    weight = factor_y * factor_z * (2.0 * full_turn)

    def scale(a, carry):
        square = plane + squares_ref[a]
        safe = jnp.where(square > 0, square, 1.0)
        green = jnp.exp(square * (-0.5 * screen_width * screen_width)) / safe
        green = jnp.where(square > 0, green, 0.0) * (weight * factors_ref[a])
        where = pl.ds(pl.multiple_of(a * modes_y, modes_y), modes_y)
        value = (spectrum_ref[where, :] * green).astype(jnp.bfloat16)
        scaled_ref[where, :modes_z] = value
        scaled_ref[where, modes_z:] = value
        return carry

    lax.fori_loop(0, modes_x, scale, 0)
    found_ref[...] = jnp.zeros_like(found_ref)

    def tile_step(tile, carry):
        lanes = pl.ds(pl.multiple_of(tile * TILE, TILE), TILE)
        y = y_ref[:, lanes]
        slope_y = slope_y_ref[:, lanes]
        z = z_ref[:, lanes]
        slope_z = slope_z_ref[:, lanes]

        def rows(g, sums):
            spot = pl.ds(pl.multiple_of(g * group, group), group)
            x = x_ref[spot, lanes]
            slope_x = slope_x_ref[spot, lanes]
            where = pl.ds(pl.multiple_of(g * group * modes_y, group * modes_y), group * modes_y)
            left = scaled_ref[where, :]
            along = jnp.dot(left, z, preferred_element_type=jnp.float32)
            slant = jnp.dot(left, slope_z, preferred_element_type=jnp.float32)
            value, field_x, field_y, field_z = sums
            for a in range(group):
                part = along[a * modes_y : (a + 1) * modes_y]
                skew = slant[a * modes_y : (a + 1) * modes_y]
                over = jnp.sum((part * y).reshape(modes_y // 8, 8, TILE), axis=0)
                tilt = jnp.sum((part * slope_y).reshape(modes_y // 8, 8, TILE), axis=0)
                deep = jnp.sum((skew * y).reshape(modes_y // 8, 8, TILE), axis=0)
                row = x[a : a + 1]
                value = value + over * row
                field_x = field_x + over * slope_x[a : a + 1]
                field_y = field_y + tilt * row
                field_z = field_z + deep * row
            return value, field_x, field_y, field_z

        zero = jnp.zeros((8, TILE), jnp.float32)
        sums = lax.fori_loop(0, modes_x // group, rows, (zero, zero, zero, zero))
        for part in range(TILE // LANES):
            for c in range(4):
                found_ref[tile * (TILE // LANES) + part, c : c + 1, :] = jnp.sum(
                    sums[c][:, part * LANES : (part + 1) * LANES], axis=0, keepdims=True
                )
        return carry

    lax.fori_loop(0, (total + TILE - 1) // TILE, tile_step, 0)
    lane = lax.broadcasted_iota(jnp.int32, (8, LANES), 1)

    def place(j, start):
        tile = start // LANES
        shift = start % LANES
        back = (LANES - shift) % LANES
        first = pltpu.roll(found_ref[tile], back, 1)
        second = pltpu.roll(found_ref[tile + 1], back, 1)
        out_ref[j] = jnp.where(lane < LANES - shift, first, second)
        return start + count_ref[j]

    lax.fori_loop(0, columns, place, 0)


def mesh_sums(counts, squares_x, factors_x, side_y, side_z, charge, tables):
    columns = counts.shape[0]
    modes_x = tables[0].shape[0]
    modes_y = tables[2].shape[0]
    modes_z = tables[4].shape[0] // 2
    vmem = pl.BlockSpec(memory_space=pltpu.VMEM)
    smem = pl.BlockSpec(memory_space=pltpu.SMEM)
    return pl.pallas_call(
        mesh_kernel,
        in_specs=[smem, smem, smem] + [vmem] * 9,
        out_specs=vmem,
        out_shape=jax.ShapeDtypeStruct((columns, 8, LANES), jnp.float32),
        scratch_shapes=[
            pltpu.VMEM((modes_x * modes_y, modes_z), jnp.float32),
            pltpu.VMEM((modes_x * modes_y, 2 * modes_z), jnp.bfloat16),
            pltpu.VMEM((tables[0].shape[1] // LANES + 2, 8, LANES), jnp.float32),
        ],
        compiler_params=pltpu.CompilerParams(vmem_limit_bytes=60 * 2**20),
    )(counts, squares_x, factors_x, side_y, side_z, charge, *tables)


def local_sites(
    positions,
    neighbours,
    live_count,
    stencil_base,
    spline_weight,
    spline_slope,
    embed_scale,
    embed_bias,
    desc_gain,
    fit_in,
    fit_bias,
    fit_hidden,
    fit_bias_two,
    fit_out,
):
    both = ("gx", "gy")
    columns_x = lax.axis_size("gx")
    columns_y = lax.axis_size("gy")
    columns = columns_x * columns_y
    place_x = lax.axis_index("gx")
    place_y = lax.axis_index("gy")
    width_x = GRID // columns_x
    width_y = GRID // columns_y
    atoms = positions.shape[3]
    origin = jnp.stack([place_x * width_x, place_y * width_y, 0])
    cells = (stencil_base[:, 0, 0, :] + origin[:, None] + 1).astype(jnp.float32)
    counted = jnp.broadcast_to(live_count.astype(jnp.float32), (1, atoms))
    parcel = jnp.concatenate(
        [
            positions[:, 0, 0, :],
            counted,
            cells,
            spline_weight[:, :, 0, 0, :].reshape(12, atoms),
            spline_slope[:, :, 0, 0, :].reshape(12, atoms),
        ],
        axis=0,
    )
    shared = lax.all_gather(parcel, both, axis=0, tiled=False)
    counts = shared[:, 3, 0].astype(jnp.int32)
    near = []
    for stride_x in (-1, 0, 1):
        for stride_y in (-1, 0, 1):
            other_x = (place_x + stride_x) % columns_x
            other_y = (place_y + stride_y) % columns_y
            block = lax.dynamic_index_in_dim(
                shared, other_x * columns_y + other_y, axis=0, keepdims=False
            )[:3]
            offset = jnp.array([stride_x * width_x, stride_y * width_y, 0], jnp.float32)
            near.append(block + offset[:, None])
    mixed = mixed_features(
        jnp.stack(near, axis=1), neighbours[:, 0, 0, :], embed_scale, embed_bias
    )
    charge = fit_charge(
        mixed, live_count[0, 0], desc_gain, fit_in, fit_bias, fit_hidden, fit_bias_two, fit_out
    )
    charges = lax.all_gather(charge, both, axis=0, tiled=False)
    sites = jnp.concatenate(
        [shared[:, 4:], charges[:, None, :], jnp.zeros((columns, 4, atoms), jnp.float32)], axis=1
    )
    packed = pack_sites(counts, sites)[:columns]
    slots = -(-(columns * atoms) // CHUNK) * CHUNK
    packed = jnp.transpose(packed, (1, 0, 2)).reshape(packed.shape[1], columns * atoms)
    packed = jnp.pad(packed, ((0, 0), (0, slots - columns * atoms)))
    cells = packed[:3].astype(jnp.int32)
    taps = packed[3:15].reshape(3, 4, -1)
    slopes = packed[15:27].reshape(3, 4, -1)
    half_x = GRID // columns_x // 2
    half_y = GRID // columns_y // 2
    start_x = place_x * half_x
    start_y = place_y * half_y
    table_x, slope_x = plane_tables(cells[0], taps[0], slopes[0], start_x, half_x // 8)
    table_y, slope_y = plane_tables(cells[1], taps[1], slopes[1], start_y, half_y // 8)
    cosine, sine = axis_waves(cells[2], 0, GRID // 16)
    table_z = halves(jnp.concatenate(axis_table(cosine, sine, taps[2], 0), axis=0))
    slope_z = halves(jnp.concatenate(axis_table(cosine, sine, slopes[2], 0), axis=0))
    squares_x, factors_x = plane_modes(start_x, half_x)
    squares_y, factors_y = plane_modes(start_y, half_y)
    mode_z = jnp.arange(GRID, dtype=jnp.int32) % (GRID // 2)
    wave_z = mode_z.astype(jnp.float32) * (full_turn / GRID)
    factors_z = jnp.where(mode_z == 0, 1.0, 2.0).astype(jnp.float32) / GRID
    side_y = jnp.stack([squares_y, factors_y], axis=1)
    side_z = jnp.stack([wave_z * wave_z, factors_z], axis=0)
    sums = mesh_sums(
        counts,
        squares_x,
        factors_x,
        side_y,
        side_z,
        packed[27:28],
        (table_x, slope_x, table_y, slope_y, table_z, slope_z),
    )
    mine = lax.psum_scatter(sums[:, :4], both, scatter_dimension=0, tiled=True)[0]
    energy = (0.5 * charge * mine[0]).reshape(1, 1, atoms)
    force = (-charge[None, :] * mine[1:]).reshape(3, 1, 1, atoms)
    return (energy, force)


def padded_2(shard, sides, width):
    for axis, dim in sides:
        peers, length = (lax.axis_size(axis), shard.shape[dim])
        up = [(i, (i + 1) % peers) for i in range(peers)]
        down = [(j, i) for i, j in up]
        last = lax.slice_in_dim(shard, length - width, length, axis=dim)
        leading = lax.slice_in_dim(shard, 0, width, axis=dim)
        before = lax.ppermute(last, axis, up)
        after = lax.ppermute(leading, axis, down)
        shard = jnp.concatenate([before, shard, after], axis=dim)
    return shard


def shifted(block, axis, distance):
    devices = range(lax.axis_size(axis))
    route = [((i - distance) % len(devices), i) for i in devices]
    return lax.ppermute(block, axis, route)


def stencil_table(anchor, weights, length, offset, periodic):
    count = anchor.shape[0]
    cell_index = lax.broadcasted_iota(jnp.int32, (4, length, count), 1)
    tap_index = lax.broadcasted_iota(jnp.int32, (4, length, count), 0)
    target = anchor[None, None, :] + tap_index + offset
    if periodic:
        target = target % length
    chosen = jnp.where(target == cell_index, weights[:, None, :], jnp.zeros((), weights.dtype))
    return jnp.sum(chosen, axis=0)


def spread_cells(charge, anchor, weights, extent_x, extent_y, offset, length):
    table_x = stencil_table(anchor[0], weights[0] * charge[None, :], extent_x, offset, False)
    table_y = stencil_table(anchor[1], weights[1], extent_y, offset, False)
    table_z = stencil_table(anchor[2], weights[2], length, 0, True)
    planes = (table_x[:, None, :] * table_y[None, :, :]).reshape(extent_x * extent_y, -1)
    return jnp.dot(planes, table_z.T, precision=highest).reshape(extent_x, extent_y, length)


def interpolate(padded, anchor, weights, slopes):
    extent_x, extent_y, length = padded.shape
    table_x = stencil_table(anchor[0], weights[0], extent_x, 2, False)
    slope_x = stencil_table(anchor[0], slopes[0], extent_x, 2, False)
    table_y = stencil_table(anchor[1], weights[1], extent_y, 2, False)
    slope_y = stencil_table(anchor[1], slopes[1], extent_y, 2, False)
    table_z = stencil_table(anchor[2], weights[2], length, 0, True)
    slope_z = stencil_table(anchor[2], slopes[2], length, 0, True)
    flat = padded.reshape(extent_x * extent_y, length)
    along = jnp.dot(flat, table_z, precision=highest).reshape(extent_x, extent_y, -1)
    slant = jnp.dot(flat, slope_z, precision=highest).reshape(extent_x, extent_y, -1)
    over_y = jnp.sum(along * table_y[None], axis=1)
    value = jnp.sum(table_x * over_y, axis=0)
    field_x = -jnp.sum(slope_x * over_y, axis=0)
    over_x = jnp.sum(along * table_x[:, None, :], axis=0)
    field_y = -jnp.sum(slope_y * over_x, axis=0)
    slant_y = jnp.sum(slant * table_y[None], axis=1)
    field_z = -jnp.sum(table_x * slant_y, axis=0)
    return (value, jnp.stack([field_x, field_y, field_z]))


def fitted_charge(
    nearby,
    listed,
    count,
    embed_scale,
    embed_bias,
    desc_gain,
    fit_in,
    fit_bias,
    fit_hidden,
    fit_bias_two,
    fit_out,
):
    atoms = listed.shape[1]
    center = nearby[:, 4 * atoms : 5 * atoms]
    picked = jnp.take(nearby, listed.reshape(-1), axis=1).reshape(3, listed.shape[0], atoms)
    delta = picked - center[:, None, :]
    radius = jnp.sqrt(jnp.sum(delta * delta, axis=0))
    smooth = 1.0 / (1.0 + radius / radius_scale)
    factor = smooth / (radius + radius_scale)
    envelope = jnp.concatenate([smooth[None], delta * factor[None]], axis=0)
    embed = jnp.tanh(smooth[None] * embed_scale[:, None, None] + embed_bias[:, None, None])
    mixed = jnp.einsum("ekn,ckn->ecn", embed, envelope, precision=highest)
    descriptor = jnp.einsum("ecn,acn->ean", mixed, mixed[:AXIS], precision=highest).reshape(
        -1, atoms
    )
    scaling = lax.rsqrt(jnp.mean(descriptor * descriptor, axis=0) + norm_floor)
    normed = (descriptor * scaling[None, :] * desc_gain[:, None]).astype(jnp.bfloat16)
    first = jnp.tanh(
        jnp.dot(fit_in, normed, preferred_element_type=jnp.float32) + fit_bias[:, None]
    )
    second = (
        jnp.tanh(
            jnp.dot(fit_hidden, first.astype(jnp.bfloat16), preferred_element_type=jnp.float32)
            + fit_bias_two[:, None]
        )
        + first
    )
    charge = jnp.sum(fit_out[:, None] * second, axis=0)
    slot_index = lax.broadcasted_iota(jnp.int32, (atoms,), 0)
    return jnp.where(slot_index < count, charge, jnp.zeros((), charge.dtype))


def wave_number(index, length):
    signed = jnp.where(index > length // 2, index - length, index)
    return signed.astype(jnp.float32) * (full_turn / length)


def green_values(index_x, index_y, index_z, length):
    wave_x = wave_number(index_x, length)
    wave_y = wave_number(index_y, length)
    wave_z = wave_number(index_z, length)
    square = wave_x * wave_x + wave_y * wave_y + wave_z * wave_z
    safe = jnp.where(square > 0, square, 1.0)
    value = 2.0 * full_turn * jnp.exp(-0.5 * screen_width * screen_width * square) / safe
    keep = (square > 0) & (index_z != length // 2)
    return jnp.where(keep, value, 0.0)


def wave_tables(length, count):
    rows = lax.broadcasted_iota(jnp.int32, (length, count), 0)
    cols = lax.broadcasted_iota(jnp.int32, (length, count), 1)
    angle = (rows * cols % length).astype(jnp.float32) * (full_turn / length)
    return (jnp.cos(angle), jnp.sin(angle))


def along_axis(real_part, imag_part, cosine, sine, sign, form):
    real_cos = jnp.einsum(form, real_part, cosine, precision=highest)
    real_sin = jnp.einsum(form, real_part, sine, precision=highest)
    imag_cos = jnp.einsum(form, imag_part, cosine, precision=highest)
    imag_sin = jnp.einsum(form, imag_part, sine, precision=highest)
    return (real_cos + sign * imag_sin, imag_cos - sign * real_sin)


def local_mesh(
    positions,
    neighbours,
    live_count,
    stencil_base,
    spline_weight,
    spline_slope,
    embed_scale,
    embed_bias,
    desc_gain,
    fit_in,
    fit_bias,
    fit_hidden,
    fit_bias_two,
    fit_out,
):
    columns_y = lax.axis_size("gy")
    width_x = GRID // lax.axis_size("gx")
    width_y = GRID // columns_y
    atoms = positions.shape[3]
    beside_all = padded_2(positions, (("gx", 1), ("gy", 2)), 1)
    block_x = lax.broadcasted_iota(jnp.int32, (3, 3, atoms), 0) - 1
    block_y = lax.broadcasted_iota(jnp.int32, (3, 3, atoms), 1) - 1
    offsets = jnp.stack([block_x * width_x, block_y * width_y, jnp.zeros_like(block_x)]).astype(
        jnp.float32
    )
    nearby = (beside_all + offsets).reshape(3, 9 * atoms)
    charge = fitted_charge(
        nearby,
        neighbours[:, 0, 0, :],
        live_count[0, 0],
        embed_scale,
        embed_bias,
        desc_gain,
        fit_in,
        fit_bias,
        fit_hidden,
        fit_bias_two,
        fit_out,
    )
    anchor = stencil_base[:, 0, 0, :]
    weights = spline_weight[:, :, 0, 0, :]
    slopes = spline_slope[:, :, 0, 0, :]
    spread = spread_cells(charge, anchor, weights, width_x + 4, width_y + 4, 2, GRID)
    inner = spread[2 : width_x + 2]
    for stride in (1, -1):
        piece = spread[width_x + 2 :] if stride == 1 else spread[:2]
        moved = shifted(piece, "gx", stride)
        if stride == 1:
            inner = inner.at[:2].add(moved)
        else:
            inner = inner.at[width_x - 2 :].add(moved)
    density = inner[:, 2 : width_y + 2]
    for stride in (1, -1):
        piece = inner[:, width_y + 2 :] if stride == 1 else inner[:, :2]
        moved = shifted(piece, "gy", stride)
        if stride == 1:
            density = density.at[:, :2].add(moved)
        else:
            density = density.at[:, width_y - 2 :].add(moved)
    freqs = GRID // 2
    fold_weight = jnp.where(jnp.arange(freqs) == 0, 1.0, 2.0).astype(jnp.float32) / GRID
    cosine_z, sine_z = wave_tables(GRID, freqs)
    flat = density.reshape(width_x * width_y, GRID)
    real_part = jnp.dot(flat, cosine_z, precision=highest).reshape(width_x, width_y, freqs)
    imag_part = -jnp.dot(flat, sine_z, precision=highest).reshape(width_x, width_y, freqs)
    real_part, imag_part = (
        lax.all_to_all(real_part, "gy", split_axis=2, concat_axis=1, tiled=True),
        lax.all_to_all(imag_part, "gy", split_axis=2, concat_axis=1, tiled=True),
    )
    cosine, sine = wave_tables(GRID, GRID)
    real_part, imag_part = along_axis(real_part, imag_part, cosine, sine, 1.0, "xym,yk->xkm")
    real_part, imag_part = (
        lax.all_to_all(real_part, "gx", split_axis=1, concat_axis=0, tiled=True),
        lax.all_to_all(imag_part, "gx", split_axis=1, concat_axis=0, tiled=True),
    )
    real_part, imag_part = along_axis(real_part, imag_part, cosine, sine, 1.0, "xym,xk->kym")
    span_y = real_part.shape[1]
    span_z = real_part.shape[2]
    index_x = lax.broadcasted_iota(jnp.int32, (GRID, span_y, span_z), 0)
    index_y = lax.axis_index("gx") * span_y + lax.broadcasted_iota(
        jnp.int32, (GRID, span_y, span_z), 1
    )
    index_z = lax.axis_index("gy") * span_z + lax.broadcasted_iota(
        jnp.int32, (GRID, span_y, span_z), 2
    )
    green = green_values(index_x, index_y, index_z, GRID)
    real_part = real_part * green
    imag_part = imag_part * green
    back_cos = cosine / GRID
    back_sin = sine / GRID
    real_part, imag_part = along_axis(real_part, imag_part, back_cos, back_sin, -1.0, "xym,xk->kym")
    real_part, imag_part = (
        lax.all_to_all(real_part, "gx", split_axis=0, concat_axis=1, tiled=True),
        lax.all_to_all(imag_part, "gx", split_axis=0, concat_axis=1, tiled=True),
    )
    real_part, imag_part = along_axis(real_part, imag_part, back_cos, back_sin, -1.0, "xym,yk->xkm")
    real_part, imag_part = (
        lax.all_to_all(real_part, "gy", split_axis=1, concat_axis=2, tiled=True),
        lax.all_to_all(imag_part, "gy", split_axis=1, concat_axis=2, tiled=True),
    )
    rows_y = real_part.shape[1]
    flat_real = real_part.reshape(width_x * rows_y, freqs)
    flat_imag = imag_part.reshape(width_x * rows_y, freqs)
    summed_cos = (cosine_z * fold_weight[None, :]).T
    summed_sin = (sine_z * fold_weight[None, :]).T
    potential = jnp.dot(flat_real, summed_cos, precision=highest) - jnp.dot(
        flat_imag, summed_sin, precision=highest
    )
    potential = potential.reshape(width_x, rows_y, GRID)
    padded = padded_2(potential, (("gx", 0), ("gy", 1)), 2)
    value, field = interpolate(padded, anchor, weights, slopes)
    energy = (0.5 * charge * value).reshape(1, 1, atoms)
    force = (charge[None, :] * field).reshape(3, 1, 1, atoms)
    return (energy, force)


def solution(mesh):
    def local(positions, *rest):
        columns_x, columns_y = (lax.axis_size("gx"), lax.axis_size("gy"))
        sites = columns_x * columns_y * positions.shape[3]
        whole = GRID % (16 * columns_x) == 0 and GRID % (16 * columns_y) == 0
        few = whole and sites <= 8 * GRID * 2
        return (local_sites if few and positions.shape[3] == LANES else local_mesh)(positions, *rest)

    placed = (
        P(None, "gx", "gy", None),
        P(None, "gx", "gy", None),
        P("gx", "gy"),
        P(None, "gx", "gy", None),
        P(None, None, "gx", "gy", None),
        P(None, None, "gx", "gy", None),
        P(),
        P(),
        P(),
        P(),
        P(),
        P(),
        P(),
        P(),
    )
    return jax.shard_map(
        local,
        mesh=mesh,
        in_specs=placed,
        out_specs=(P("gx", "gy", None), P(None, "gx", "gy", None)),
        check_vma=False,
    )
```
